32 devices in a mesh: leaf: 16 (over z, x, core), rhs: 2 (over y).
Axes of the slice: x: 2, y: 2, z: 4, core: 2. Of those that a mesh axis runs over, the one named last changes fastest.
Arguments:
- rhs: bfloat16 [131072, 512], P('leaf', 'rhs'), may hold values from -6 to 6
- source_basis: bfloat16 [1024, 128, 128], P('leaf', None, 'rhs'), may hold values from -0.5 to 0.5
- target_basis: bfloat16 [1024, 128, 128], P('leaf', None, 'rhs'), may hold values from -0.5 to 0.5
- near_blocks: bfloat16 [1024, 2, 128, 128], P('leaf', None, None, 'rhs'), may hold values from -0.375 to 0.375
- near_offsets: int32 [1024, 2], P('leaf'), may hold values from -2 to 2
- source_values: bfloat16 [3, 512, 2, 2, 128, 128], P(None, 'leaf', None, None, 'rhs'), may hold values from -0.375 to 0.375
- source_scales: float32 [3, 512, 2, 2, 128], P(None, 'leaf'), may hold values from 0.2 to 2
- target_values: bfloat16 [3, 512, 2, 2, 128, 128], P(None, 'leaf', None, None, 'rhs'), may hold values from -0.375 to 0.375
- target_scales: float32 [3, 512, 2, 2, 128], P(None, 'leaf'), may hold values from 0.2 to 2
Outputs:
- product: bfloat16 [131072, 512], P('leaf', 'rhs')
The draws below stay inside these ranges and needn't reach their ends.
All inputs are finite; a program needn't handle non-finite values.
Results may differ from the reference program's by a relative error of at most 0.01.
Values may be sent and summed in bfloat16 or wider, within the bound.
No kernel may reach another device: no remote copies, remote signals or barrier semaphores. Data moves between devices by JAX's collectives and lax.ppermute only.
A program may use at most 192 MiB of HBM per device.

```python
import math
import jax
import jax.numpy as jnp
from jax import lax

M = 128
R = 128
BOX_DEV = 64
K = 2
REACH = 2
SRC_LEVELS = 3
TGT_LEVELS = 3
BOXES = 1024
ORDER = 131072
RHS = 512
N_LEAF = 16


def plant(values, rng, low, top_value):
    extent = values.shape
    spot = [jax.random.randint(jax.random.fold_in(rng, axis), (), 0, extent[axis]) for axis in range(len(extent))]
    values = values.at[tuple(spot)].set(low)
    longest = extent.index(max(extent))
    spot[longest] = (spot[longest] + 1) % extent[longest]
    return values.at[tuple(spot)].set(top_value)


def levels(stream_key, dims, shards, smallest, top_value):
    factor_of, own = 1.0, jax.random.fold_in(stream_key, 6)
    for dim, shards_of in shards:
        draws = jnp.exp(jax.random.uniform(jax.random.fold_in(own, dim), (shards_of,), jnp.float32, smallest / len(shards), top_value / len(shards)))
        factor_of = factor_of * jnp.repeat(draws, dims[dim] // shards_of).reshape([-1 if axis == dim else 1 for axis in range(len(dims))])
    return factor_of


def scatter_about(stream_key, dims, scale, limit, cuts=(), kind=jnp.bfloat16):
    result = jax.random.normal(stream_key, dims, jnp.float32) * scale
    if len(cuts) > 0:
        result = levels(stream_key, dims, cuts, -0.22, 0.18) * result
    return jnp.clip(result, min=-limit, max=limit).astype(kind)


def setup_inputs(seed: int = 0) -> dict:
    key_list = jax.random.split(jax.random.key(seed), 10)
    return {
        "rhs": scatter_about(key_list[0], (ORDER, RHS), 1.0, 6.0, ((0, 16), (1, 2))),
        "source_basis": scatter_about(key_list[1], (BOXES, M, R), M ** -0.5, 0.5, ((0, 16), (2, 2))),
        "target_basis": scatter_about(key_list[2], (BOXES, M, R), R ** -0.5, 0.5, ((0, 16), (2, 2))),
        "near_blocks": scatter_about(key_list[3], (BOXES, K, M, M), (K * M) ** -0.5, 0.375, ((0, 16), (3, 2))),
        "near_offsets": plant(jax.random.randint(key_list[4], (BOXES, K), -REACH, REACH + 1), jax.random.fold_in(key_list[4], 1), -REACH, REACH).astype(jnp.int32),
        "source_values": scatter_about(key_list[5], (SRC_LEVELS, BOXES // 2, 2, 2, R, R), (2 * R) ** -0.5, 0.375, ((1, 16), (4, 2))),
        "source_scales": jnp.clip(jnp.exp(math.log(2.0) - 2.3025851 * jax.random.uniform(key_list[6], (SRC_LEVELS, BOXES // 2, 2, 2, R), jnp.float32) ** levels(key_list[6], (SRC_LEVELS, BOXES // 2, 2, 2, R), ((1, 16),), -0.2, 0.2)), 0.2, 2.0),
        "target_values": scatter_about(key_list[7], (TGT_LEVELS, BOXES // 2, 2, 2, R, R), (2 * R) ** -0.5, 0.375, ((1, 16), (4, 2))),
        "target_scales": jnp.clip(jnp.exp(math.log(2.0) - 2.3025851 * jax.random.uniform(key_list[8], (TGT_LEVELS, BOXES // 2, 2, 2, R), jnp.float32) ** levels(key_list[8], (TGT_LEVELS, BOXES // 2, 2, 2, R), ((1, 16),), -0.2, 0.2)), 0.2, 2.0),
    }


def dequantize(values, scales):
    return (values.astype(jnp.float32) * scales[..., None, :]).astype(jnp.bfloat16)


def butterfly_level(coefficients, blocks, bit_index):
    box_total, columns, rank = coefficients.shape
    outputs = blocks.shape[-2]
    low_span = 2 ** bit_index
    high_span = box_total // (2 * low_span)
    inputs = coefficients.reshape(high_span, 2, low_span, columns, rank).astype(jnp.float32)
    matrices = blocks.reshape(high_span, low_span, 2, 2, outputs, rank).astype(jnp.float32)
    mixed = jnp.einsum("hclnr,hlocsr->holns", inputs, matrices)
    return mixed.reshape(box_total, columns, outputs).astype(jnp.bfloat16)


def reference(rhs, source_basis, target_basis, near_blocks, near_offsets, source_values, source_scales, target_values, target_scales):
    box_total = BOX_DEV * N_LEAF
    quota_boxes = BOX_DEV // N_LEAF
    columns = math.gcd(RHS, 128)
    col_groups = RHS // columns
    source_index = jnp.arange(box_total, dtype=jnp.int32)[:, None] + REACH + near_offsets.astype(jnp.int32)

    def one_group(block_rhs):
        rhs_boxes = block_rhs.reshape(box_total, M, columns)
        coefficients = jnp.einsum("bmc,bmr->bcr", rhs_boxes.astype(jnp.float32), source_basis.astype(jnp.float32)).astype(jnp.bfloat16)
        for level_index in range(SRC_LEVELS):
            coefficients = butterfly_level(coefficients, dequantize(source_values[level_index], source_scales[level_index]), level_index)
        coefficients = coefficients.reshape(N_LEAF, N_LEAF, quota_boxes, columns, R).transpose(1, 0, 2, 3, 4).reshape(box_total, columns, R)
        for level_index in range(TGT_LEVELS):
            coefficients = butterfly_level(coefficients, dequantize(target_values[level_index], target_scales[level_index]), level_index)
        far_field = jnp.einsum("bmr,bcr->bmc", target_basis.astype(jnp.float32), coefficients.astype(jnp.float32))
        padded = jnp.pad(rhs_boxes, ((REACH, REACH), (0, 0), (0, 0)))
        selected = jnp.take(padded, source_index, axis=0)
        near_field = jnp.einsum("bkmn,bknc->bmc", near_blocks.astype(jnp.float32), selected.astype(jnp.float32))
        return (far_field + near_field).astype(jnp.bfloat16).reshape(box_total * M, columns)

    grouped = rhs.reshape(box_total * M, col_groups, columns).transpose(1, 0, 2)
    results = lax.map(one_group, grouped)
    return results.transpose(1, 0, 2).reshape(box_total * M, RHS)
```

```python
import functools

import jax
import jax.numpy as jnp
from jax import lax
from jax.experimental import pallas as pl
from jax.experimental.pallas import tpu as pltpu
from jax.sharding import PartitionSpec as P

REACH = 2
SWAP = [(0, 1), (1, 0)]


def parity(value):
    return bin(value).count("1") & 1


def fill_level(weights, own, peer, scales, level, pairs, half, low, high):
    width = scales.shape[-1]
    for p in range(pairs):
        for o in range(2):
            for c in range(2):
                scale = scales[level, p, o, c : c + 1, :]
                for part, at in ((own, low), (peer, high)):
                    block = (part[level, p, o, c].astype(jnp.float32) * scale).astype(jnp.bfloat16)
                    start = pl.multiple_of(o * 2 * half + at, half)
                    weights[p, pl.ds(start, half), c * width : (c + 1) * width] = block


def mix_level(weights, read, write, level, pairs, rank):
    step = 2**level
    for p in range(pairs):
        i = (p >> level) * 2 * step + (p & (step - 1))
        j = i + step
        both = jnp.concatenate([read(i), read(j)], axis=0)
        mixed = jnp.dot(weights[p], both, preferred_element_type=jnp.float32).astype(jnp.bfloat16)
        write(i, mixed[:rank])
        write(j, mixed[rank:])


def source_kernel(idx, rhs_own, rhs_peer, basis_own, basis_peer, own, peer, scales, out, weights, state):
    boxes, rank, _ = out.shape
    rows = basis_own.shape[2]
    half = basis_own.shape[1]
    levels = own.shape[0]
    pairs = boxes // 2
    low = idx[1] * half
    high = (1 - idx[1]) * half
    for b in range(boxes):
        here = pl.ds(b * rows, rows)
        box = jnp.concatenate([rhs_own[here, :], rhs_peer[here, :]], axis=1)
        for part, at in ((basis_own, low), (basis_peer, high)):
            start = pl.multiple_of(b * rank + at, half)
            state[pl.ds(start, half), :] = jnp.dot(
                part[b], box, preferred_element_type=jnp.float32
            ).astype(jnp.bfloat16)

    def read(i):
        return state[i * rank : (i + 1) * rank, :]

    def write_state(i, value):
        state[i * rank : (i + 1) * rank, :] = value

    def write_out(i, value):
        out[i] = value

    for level in range(levels):
        fill_level(weights, own, peer, scales, level, pairs, half, low, high)
        mix_level(weights, read, write_out if level == levels - 1 else write_state, level, pairs, rank)


def target_kernel(
    idx, offsets, mixed, own, peer, scales, basis_own, basis_peer, near_own, near_peer, win_own, win_peer,
    *rest, first,
):
    prod, send, weights, state, left = rest if first else rest[1:]
    boxes, rank, _ = mixed.shape
    half = basis_own.shape[1]
    rows = basis_own.shape[2]
    near_count = near_own.shape[1]
    levels = own.shape[0]
    pairs = boxes // 2
    columns = prod.shape[1]
    low = idx[1] * half
    high = (1 - idx[1]) * half
    step = pl.program_id(0)

    def read_in(i):
        return mixed[i]

    def read_state(i):
        return state[i * rank : (i + 1) * rank, :]

    def write_state(i, value):
        state[i * rank : (i + 1) * rank, :] = value

    for level in range(levels):
        fill_level(weights, own, peer, scales, level, pairs, half, low, high)
        mix_level(weights, read_state if level else read_in, write_state, level, pairs, rank)
    first_box = idx[0] * boxes * pl.num_programs(0) + step * boxes
    for b in range(boxes):
        parts = [read_state(b)]
        for k in range(near_count):
            at = (step * boxes + b + REACH + offsets[(first_box + b) * near_count + k]) * rows
            there = pl.ds(pl.multiple_of(at, rows), rows)
            parts.append(jnp.concatenate([win_own[there, :], win_peer[there, :]], axis=1))
        for k in range(near_count + 1):
            for basis, near, at in ((basis_own, near_own, low), (basis_peer, near_peer, high)):
                start = pl.multiple_of(k * 2 * half + at, half)
                left[b, pl.ds(start, half), :] = near[b, k - 1] if k else basis[b]
        right = jnp.concatenate(parts, axis=0)
        total = lax.dot_general(
            left[b], right, (((0,), (0,)), ((), ())), preferred_element_type=jnp.float32
        ).astype(jnp.bfloat16)
        here = pl.ds(b * rows, rows)
        prod[here, :] = total[:, :columns]
        send[here, :] = total[:, columns:]


def on_device(
    rhs,
    source_basis,
    target_basis,
    near_blocks,
    near_offsets,
    source_values,
    source_scales,
    target_values,
    target_scales,
):
    leafs = lax.axis_size("leaf")
    box_count, rows, half = source_basis.shape
    columns = rhs.shape[1]
    levels = source_values.shape[0]
    rank = source_values.shape[5]
    near_count = near_blocks.shape[1]
    group = 2**levels
    chunk = 2 * group
    chunks = box_count // chunk
    quota = box_count // leafs
    span = chunk // quota
    bits = span.bit_length() - 1
    steps = chunks // 2
    masks = [[m for m in range(chunks - 1, -1, -1) if parity(m) == h] for h in range(2)]

    d = lax.axis_index("leaf")
    h = lax.axis_index("rhs")
    home = d >> bits
    mine = [home ^ jnp.where(h == 0, masks[0][s], masks[1][s]) for s in range(steps)]
    others = [home ^ jnp.where(h == 0, masks[1][s], masks[0][s]) for s in range(steps)]
    home_parity = sum(((home >> k) & 1) for k in range(chunks.bit_length())) & 1

    source_t = jnp.swapaxes(source_basis, 1, 2)
    target_t = jnp.swapaxes(target_basis, 1, 2)
    near_t = jnp.swapaxes(near_blocks, 2, 3)

    def cut(array, at, size, axis=0):
        return lax.dynamic_slice_in_dim(array, at * size, size, axis)

    def swap(array):
        return lax.ppermute(array, "rhs", SWAP)

    half_pairs = chunk // 2
    rhs_in, source_in, blocks_in = [], [], []
    for s in range(steps):
        rhs_in.append(swap(cut(rhs, others[s], chunk * rows)))
        source_in.append(swap(cut(source_t, others[s], chunk)))
        blocks_in.append(swap(cut(source_values, others[s], half_pairs, 1)))

    edges = [i for i in range(chunks - 1) if parity(i) != parity(i + 1)]
    owns = [(home_parity ^ parity(i)) == h for i in edges]
    give = [(i + 1) * chunk - jnp.where(own, REACH, 0) for i, own in zip(edges, owns)]
    take = [(i + 1) * chunk + jnp.where(own, 0, -REACH) for i, own in zip(edges, owns)]
    reach_rows = REACH * rows
    inner = swap(
        jnp.concatenate([lax.dynamic_slice_in_dim(rhs, g * rows, reach_rows, 0) for g in give], axis=0)
    )
    target_in, target_blocks_in, near_in = [], [], []
    for s in range(steps):
        target_blocks_in.append(swap(cut(target_values, others[s], half_pairs, 1)))
        target_in.append(swap(cut(target_t, others[s], chunk)))
        near_in.append(swap(cut(near_t, others[s], chunk)))

    peer_rhs = jnp.zeros(((box_count + 2 * REACH) * rows, columns), rhs.dtype)
    for s in range(steps):
        peer_rhs = lax.dynamic_update_slice_in_dim(
            peer_rhs, rhs_in[s], mine[s] * (chunk * rows) + reach_rows, 0
        )
    for n, t in enumerate(take):
        peer_rhs = lax.dynamic_update_slice_in_dim(
            peer_rhs, inner[n * reach_rows : (n + 1) * reach_rows], t * rows + reach_rows, 0
        )
    up = [(i, i + 1) for i in range(leafs - 1)]
    down = [(i + 1, i) for i in range(leafs - 1)]
    tail = rhs[-reach_rows:]
    head = rhs[:reach_rows]
    own_rhs = jnp.concatenate(
        [lax.ppermute(tail, "leaf", up), rhs, lax.ppermute(head, "leaf", down)], axis=0
    )
    peer_tail = peer_rhs[box_count * rows : box_count * rows + reach_rows]
    peer_head = peer_rhs[reach_rows : 2 * reach_rows]

    def side(device):
        return parity(device >> bits)

    def same_side(other):
        return (sum((((other >> bits) >> k) & 1) for k in range(chunks.bit_length())) & 1) == home_parity

    both = ("leaf", "rhs")
    low_peer = lax.ppermute(
        jnp.where(same_side(d + 1), peer_tail, tail), both,
        [(2 * a + side(a), 2 * b + side(b)) for a, b in up],
    )
    high_peer = lax.ppermute(
        jnp.where(same_side(d - 1), peer_head, head), both,
        [(2 * a + side(a), 2 * b + side(b)) for a, b in down],
    )
    peer_rhs = lax.dynamic_update_slice_in_dim(peer_rhs, low_peer, 0, 0)
    peer_rhs = lax.dynamic_update_slice_in_dim(peer_rhs, high_peer, box_count * rows + reach_rows, 0)

    params = pltpu.CompilerParams(
        dimension_semantics=("arbitrary",), vmem_limit_bytes=56 * 2**20
    )
    pair_count = group // 2
    wide = 2 * columns
    blocks_own = pl.BlockSpec(
        (levels, pair_count, 2, 2, half, rank), lambda t, i, *_: (0, i[0] * 2 + t, 0, 0, 0, 0)
    )
    blocks_peer = pl.BlockSpec((levels, pair_count, 2, 2, half, rank), lambda t, *_: (0, t, 0, 0, 0, 0))
    scale_spec = pl.BlockSpec(
        (levels, pair_count, 2, 2, rank), lambda t, i, *_: (0, i[0] * 2 + t, 0, 0, 0)
    )
    basis_own = pl.BlockSpec((group, half, rows), lambda t, i, *_: (i[0] * 2 + t, 0, 0))
    basis_peer = pl.BlockSpec((group, half, rows), lambda t, *_: (t, 0, 0))
    near_own = pl.BlockSpec((group, near_count, half, rows), lambda t, i, *_: (i[0] * 2 + t, 0, 0, 0))
    near_peer = pl.BlockSpec((group, near_count, half, rows), lambda t, *_: (t, 0, 0, 0))
    state_spec = pl.BlockSpec((group, rank, wide), lambda t, *_: (t, 0, 0))
    rhs_own = pl.BlockSpec((group * rows, columns), lambda t, i, *_: (i[0] * 2 + t, 0))
    rhs_peer = pl.BlockSpec((group * rows, columns), lambda t, *_: (t, 0))
    window_rows = (chunk + 2 * REACH) * rows
    window = pl.BlockSpec((window_rows, columns), lambda t, *_: (0, 0))
    weight_scratch = pltpu.VMEM((pair_count, 2 * rank, 2 * rank), rhs.dtype)
    state_scratch = pltpu.VMEM((group * rank, wide), rhs.dtype)

    rows_in = []
    for s in range(steps):
        index = jnp.stack([mine[s], h]).astype(jnp.int32)
        mixed = pl.pallas_call(
            source_kernel,
            out_shape=jax.ShapeDtypeStruct((chunk, rank, wide), rhs.dtype),
            grid_spec=pltpu.PrefetchScalarGridSpec(
                num_scalar_prefetch=1,
                grid=(2,),
                in_specs=[rhs_own, rhs_peer, basis_own, basis_peer, blocks_own, blocks_peer, scale_spec],
                out_specs=state_spec,
                scratch_shapes=[weight_scratch, state_scratch],
            ),
            compiler_params=params,
            name=f"source_{s}",
        )(index, rhs, rhs_in[s], source_t, source_in[s], source_values, blocks_in[s], source_scales)
        arrived = jnp.zeros((chunk, rank, wide), rhs.dtype)
        for k in range(span):
            slot = (d ^ k) & (span - 1)
            pairs = [
                (2 * a + e, 2 * (a ^ ((masks[e][s] << bits) | k)) + e) for a in range(leafs) for e in range(2)
            ]
            piece = lax.ppermute(cut(mixed, slot, quota), both, pairs)
            arrived = lax.dynamic_update_slice_in_dim(arrived, piece, slot * quota, 0)
        rows_in.append(arrived)

    offsets = near_offsets.reshape(-1)
    product = None
    returned = []
    for s in range(steps):
        index = jnp.stack([mine[s], h]).astype(jnp.int32)
        start = mine[s] * (chunk * rows)
        operands = [
            index, offsets, rows_in[s], target_values, target_blocks_in[s], target_scales,
            target_t, target_in[s], near_t, near_in[s],
            lax.dynamic_slice_in_dim(own_rhs, start, window_rows, 0),
            lax.dynamic_slice_in_dim(peer_rhs, start, window_rows, 0),
        ]
        specs = [
            state_spec, blocks_own, blocks_peer, scale_spec, basis_own, basis_peer, near_own, near_peer,
            window, window,
        ]
        aliases = {}
        if s:
            aliases = {len(operands): 0}
            operands.append(product)
            specs.append(pl.BlockSpec(memory_space=pl.ANY))
        product, send = pl.pallas_call(
            functools.partial(target_kernel, first=s == 0),
            out_shape=(
                jax.ShapeDtypeStruct((box_count * rows, columns), rhs.dtype),
                jax.ShapeDtypeStruct((chunk * rows, columns), rhs.dtype),
            ),
            grid_spec=pltpu.PrefetchScalarGridSpec(
                num_scalar_prefetch=2,
                grid=(2,),
                in_specs=specs,
                out_specs=(rhs_own, rhs_peer),
                scratch_shapes=[
                    weight_scratch,
                    state_scratch,
                    pltpu.VMEM((group, (near_count + 1) * 2 * half, rows), rhs.dtype),
                ],
            ),
            input_output_aliases=aliases,
            compiler_params=params,
            name=f"target_{s}",
        )(*operands)
        returned.append(swap(send))
    for s in range(steps):
        product = lax.dynamic_update_slice_in_dim(product, returned[s], others[s] * (chunk * rows), 0)
    return product


def solution(mesh):
    placed = (
        P("leaf", "rhs"),
        P("leaf", None, "rhs"),
        P("leaf", None, "rhs"),
        P("leaf", None, None, "rhs"),
        P("leaf", None),
        P(None, "leaf", None, None, "rhs", None),
        P(None, "leaf", None, None, None),
        P(None, "leaf", None, None, "rhs", None),
        P(None, "leaf", None, None, None),
    )
    return jax.shard_map(
        on_device, mesh=mesh, in_specs=placed, out_specs=P("leaf", "rhs"), check_vma=False
    )
```

```python
import functools

import jax
import jax.numpy as jnp
from jax import lax
from jax.experimental import pallas as pl
from jax.experimental.pallas import tpu as pltpu
from jax.sharding import PartitionSpec as P

REACH = 2
SWAP = [(0, 1), (1, 0)]


def parity(value):
    return bin(value).count("1") & 1


def fill_level(weights, own, peer, scales, level, pairs, half, low, high):
    width = scales.shape[-1]
    for p in range(pairs):
        for o in range(2):
            for c in range(2):
                scale = scales[level, p, o, c : c + 1, :]
                for part, at in ((own, low), (peer, high)):
                    block = (part[level, p, o, c].astype(jnp.float32) * scale).astype(jnp.bfloat16)
                    start = pl.multiple_of(o * 2 * half + at, half)
                    weights[p, pl.ds(start, half), c * width : (c + 1) * width] = block


def mix_level(weights, read, write, level, pairs, rank):
    step = 2**level
    for p in range(pairs):
        i = (p >> level) * 2 * step + (p & (step - 1))
        j = i + step
        both = jnp.concatenate([read(i), read(j)], axis=0)
        mixed = jnp.dot(weights[p], both, preferred_element_type=jnp.float32).astype(jnp.bfloat16)
        write(i, mixed[:rank])
        write(j, mixed[rank:])


def source_kernel(idx, rhs_own, rhs_peer, basis_own, basis_peer, own, peer, scales, out, weights, state):
    boxes, rank, _ = out.shape
    rows = basis_own.shape[2]
    half = basis_own.shape[1]
    levels = own.shape[0]
    pairs = boxes // 2
    low = idx[1] * half
    high = (1 - idx[1]) * half
    for b in range(boxes):
        here = pl.ds(b * rows, rows)
        box = jnp.concatenate([rhs_own[here, :], rhs_peer[here, :]], axis=1)
        for part, at in ((basis_own, low), (basis_peer, high)):
            start = pl.multiple_of(b * rank + at, half)
            state[pl.ds(start, half), :] = jnp.dot(
                part[b], box, preferred_element_type=jnp.float32
            ).astype(jnp.bfloat16)

    def read(i):
        return state[i * rank : (i + 1) * rank, :]

    def write_state(i, value):
        state[i * rank : (i + 1) * rank, :] = value

    def write_out(i, value):
        out[i] = value

    for level in range(levels):
        fill_level(weights, own, peer, scales, level, pairs, half, low, high)
        mix_level(weights, read, write_out if level == levels - 1 else write_state, level, pairs, rank)


def target_kernel(
    idx, offsets, mixed, own, peer, scales, basis_own, basis_peer, near_own, near_peer, win_own, win_peer,
    *rest, first,
):
    prod, send, weights, state, left = rest if first else rest[1:]
    boxes, rank, _ = mixed.shape
    half = basis_own.shape[1]
    rows = basis_own.shape[2]
    near_count = near_own.shape[1]
    levels = own.shape[0]
    pairs = boxes // 2
    columns = prod.shape[1]
    low = idx[1] * half
    high = (1 - idx[1]) * half
    step = pl.program_id(0)

    def read_in(i):
        return mixed[i]

    def read_state(i):
        return state[i * rank : (i + 1) * rank, :]

    def write_state(i, value):
        state[i * rank : (i + 1) * rank, :] = value

    for level in range(levels):
        fill_level(weights, own, peer, scales, level, pairs, half, low, high)
        mix_level(weights, read_state if level else read_in, write_state, level, pairs, rank)
    first_box = idx[0] * boxes * pl.num_programs(0) + step * boxes
    for b in range(boxes):
        parts = [read_state(b)]
        for k in range(near_count):
            at = (step * boxes + b + REACH + offsets[(first_box + b) * near_count + k]) * rows
            there = pl.ds(pl.multiple_of(at, rows), rows)
            parts.append(jnp.concatenate([win_own[there, :], win_peer[there, :]], axis=1))
        for k in range(near_count + 1):
            for basis, near, at in ((basis_own, near_own, low), (basis_peer, near_peer, high)):
                start = pl.multiple_of(k * 2 * half + at, half)
                left[b, pl.ds(start, half), :] = near[b, k - 1] if k else basis[b]
        right = jnp.concatenate(parts, axis=0)
        total = lax.dot_general(
            left[b], right, (((0,), (0,)), ((), ())), preferred_element_type=jnp.float32
        ).astype(jnp.bfloat16)
        here = pl.ds(b * rows, rows)
        prod[here, :] = total[:, :columns]
        send[here, :] = total[:, columns:]


def edge_kernel(meta, near_own, near_peer, *rest):
    *boxes, out = rest
    half = near_own.shape[2]
    count = pl.num_programs(0)
    j = pl.program_id(0)
    h = meta[0]
    total = jnp.zeros(out.shape, jnp.float32)
    for k, box in enumerate(boxes):
        part = jnp.zeros(out.shape, jnp.float32)
        for near, at in ((near_own, h * half), (near_peer, (1 - h) * half)):
            part += lax.dot_general(
                near[0, k], box[pl.ds(pl.multiple_of(at, half), half), :], (((0,), (0,)), ((), ())),
                preferred_element_type=jnp.float32,
            )
        reads = meta[1 + count + (len(boxes) + k) * count + j]
        total += jnp.where(reads > 0, part, 0.0)
    out[...] = total


def on_device(
    rhs,
    source_basis,
    target_basis,
    near_blocks,
    near_offsets,
    source_values,
    source_scales,
    target_values,
    target_scales,
):
    leafs = lax.axis_size("leaf")
    box_count, rows, half = source_basis.shape
    columns = rhs.shape[1]
    levels = source_values.shape[0]
    rank = source_values.shape[5]
    near_count = near_blocks.shape[1]
    group = 2**levels
    chunk = 2 * group
    chunks = box_count // chunk
    quota = box_count // leafs
    span = chunk // quota
    bits = span.bit_length() - 1
    steps = chunks // 2
    masks = [[m for m in range(chunks - 1, -1, -1) if parity(m) == h] for h in range(2)]

    d = lax.axis_index("leaf")
    h = lax.axis_index("rhs")
    home = d >> bits
    mine = [home ^ jnp.where(h == 0, masks[0][s], masks[1][s]) for s in range(steps)]
    others = [home ^ jnp.where(h == 0, masks[1][s], masks[0][s]) for s in range(steps)]
    home_parity = sum(((home >> k) & 1) for k in range(chunks.bit_length())) & 1

    source_t = jnp.swapaxes(source_basis, 1, 2)
    target_t = jnp.swapaxes(target_basis, 1, 2)
    near_t = jnp.swapaxes(near_blocks, 2, 3)

    def cut(array, at, size, axis=0):
        return lax.dynamic_slice_in_dim(array, at * size, size, axis)

    def swap(array):
        return lax.ppermute(array, "rhs", SWAP)

    edges = [i for i in range(chunks - 1) if parity(i) != parity(i + 1)]
    assert edges == list(range(0, chunks, 2))
    owns = [(home_parity ^ parity(i)) == h for i in edges]
    give = [(i + 1) * chunk - jnp.where(own, REACH, 0) for i, own in zip(edges, owns)]
    take = [(i + 1) * chunk - jnp.where(own, 0, REACH) for i, own in zip(edges, owns)]
    reach_rows = REACH * rows

    half_pairs = chunk // 2
    pool = {
        "rhs": (rhs, chunk * rows, 0),
        "source": (source_t, chunk, 0),
        "source_blocks": (source_values, half_pairs, 1),
        "target": (target_t, chunk, 0),
        "target_blocks": (target_values, half_pairs, 1),
        "near": (near_t, chunk, 0),
    }
    arrays = {name: entry[0] for name, entry in pool.items()}
    queue = [(name, s) for s in range(steps) for name in ("source", "rhs", "source_blocks")]
    for s in range(steps):
        queue += [(name, s) for name in ("target_blocks", "target", "near")] + ([] if s else ["edges"])
    received = {}
    for entry in queue:
        if entry == "edges":
            piece = jnp.concatenate(
                [lax.dynamic_slice_in_dim(arrays["near"], g, REACH, 0) for g in give], axis=0
            )
        else:
            name, s = entry
            piece = cut(arrays[name], others[s], pool[name][1], pool[name][2])
        piece, arrays = lax.optimization_barrier((piece, arrays))
        received[entry] = swap(piece)

    peer_rhs = jnp.zeros(((box_count + 2 * REACH) * rows, columns), rhs.dtype)
    for s in range(steps):
        peer_rhs = lax.dynamic_update_slice_in_dim(
            peer_rhs, received["rhs", s], mine[s] * (chunk * rows) + reach_rows, 0
        )
    peer_tail = peer_rhs[box_count * rows : box_count * rows + reach_rows]
    peer_head = peer_rhs[reach_rows : 2 * reach_rows]
    up = [(i, i + 1) for i in range(leafs - 1)]
    down = [(i + 1, i) for i in range(leafs - 1)]
    tail = rhs[-reach_rows:]
    head = rhs[:reach_rows]

    def side(device):
        return parity(device >> bits)

    def same_side(other):
        return (sum((((other >> bits) >> k) & 1) for k in range(chunks.bit_length())) & 1) == home_parity

    both = ("leaf", "rhs")
    low_peer = lax.ppermute(
        jnp.where(same_side(d + 1), peer_tail, tail), both,
        [(2 * a + side(a), 2 * b + side(b)) for a, b in up],
    )
    high_peer = lax.ppermute(
        jnp.where(same_side(d - 1), peer_head, head), both,
        [(2 * a + side(a), 2 * b + side(b)) for a, b in down],
    )
    peer_rhs = lax.dynamic_update_slice_in_dim(peer_rhs, low_peer, 0, 0)
    peer_rhs = lax.dynamic_update_slice_in_dim(peer_rhs, high_peer, box_count * rows + reach_rows, 0)
    own_rhs = jnp.concatenate(
        [lax.ppermute(tail, "leaf", up), rhs, lax.ppermute(head, "leaf", down)], axis=0
    )

    params = pltpu.CompilerParams(
        dimension_semantics=("arbitrary",), vmem_limit_bytes=56 * 2**20
    )
    pair_count = group // 2
    wide = 2 * columns
    blocks_own = pl.BlockSpec(
        (levels, pair_count, 2, 2, half, rank), lambda t, i, *_: (0, i[0] * 2 + t, 0, 0, 0, 0)
    )
    blocks_peer = pl.BlockSpec((levels, pair_count, 2, 2, half, rank), lambda t, *_: (0, t, 0, 0, 0, 0))
    scale_spec = pl.BlockSpec(
        (levels, pair_count, 2, 2, rank), lambda t, i, *_: (0, i[0] * 2 + t, 0, 0, 0)
    )
    basis_own = pl.BlockSpec((group, half, rows), lambda t, i, *_: (i[0] * 2 + t, 0, 0))
    basis_peer = pl.BlockSpec((group, half, rows), lambda t, *_: (t, 0, 0))
    near_own = pl.BlockSpec((group, near_count, half, rows), lambda t, i, *_: (i[0] * 2 + t, 0, 0, 0))
    near_peer = pl.BlockSpec((group, near_count, half, rows), lambda t, *_: (t, 0, 0, 0))
    state_spec = pl.BlockSpec((group, rank, wide), lambda t, *_: (t, 0, 0))
    rhs_own = pl.BlockSpec((group * rows, columns), lambda t, i, *_: (i[0] * 2 + t, 0))
    rhs_peer = pl.BlockSpec((group * rows, columns), lambda t, *_: (t, 0))
    window_rows = (chunk + 2 * REACH) * rows
    window = pl.BlockSpec((window_rows, columns), lambda t, *_: (0, 0))
    weight_scratch = pltpu.VMEM((pair_count, 2 * rank, 2 * rank), rhs.dtype)
    state_scratch = pltpu.VMEM((group * rank, wide), rhs.dtype)

    rows_in = []
    for s in range(steps):
        index = jnp.stack([mine[s], h]).astype(jnp.int32)
        mixed = pl.pallas_call(
            source_kernel,
            out_shape=jax.ShapeDtypeStruct((chunk, rank, wide), rhs.dtype),
            grid_spec=pltpu.PrefetchScalarGridSpec(
                num_scalar_prefetch=1,
                grid=(2,),
                in_specs=[rhs_own, rhs_peer, basis_own, basis_peer, blocks_own, blocks_peer, scale_spec],
                out_specs=state_spec,
                scratch_shapes=[weight_scratch, state_scratch],
            ),
            compiler_params=params,
        )(index, rhs, received["rhs", s], source_t, received["source", s], source_values, received["source_blocks", s], source_scales)
        arrived = jnp.zeros((chunk, rank, wide), rhs.dtype)
        for k in range(span):
            slot = (d ^ k) & (span - 1)
            pairs = [
                (2 * a + e, 2 * (a ^ ((masks[e][s] << bits) | k)) + e) for a in range(leafs) for e in range(2)
            ]
            piece = lax.ppermute(cut(mixed, slot, quota), both, pairs)
            arrived = lax.dynamic_update_slice_in_dim(arrived, piece, slot * quota, 0)
        rows_in.append(arrived)

    offsets = near_offsets.reshape(-1)
    product = None
    returned = []
    for s in range(steps):
        index = jnp.stack([mine[s], h]).astype(jnp.int32)
        start = mine[s] * (chunk * rows)
        operands = [
            index, offsets, rows_in[s], target_values, received["target_blocks", s], target_scales,
            target_t, received["target", s], near_t, received["near", s],
            lax.dynamic_slice_in_dim(own_rhs, start, window_rows, 0),
            lax.dynamic_slice_in_dim(peer_rhs, start, window_rows, 0),
        ]
        specs = [
            state_spec, blocks_own, blocks_peer, scale_spec, basis_own, basis_peer, near_own, near_peer,
            window, window,
        ]
        aliases = {}
        if s:
            aliases = {len(operands): 0}
            operands.append(product)
            specs.append(pl.BlockSpec(memory_space=pl.ANY))
        far = pl.pallas_call(
            functools.partial(target_kernel, first=s == 0),
            out_shape=(
                jax.ShapeDtypeStruct((box_count * rows, columns), rhs.dtype),
                jax.ShapeDtypeStruct((chunk * rows, columns), rhs.dtype),
            ),
            grid_spec=pltpu.PrefetchScalarGridSpec(
                num_scalar_prefetch=2,
                grid=(2,),
                in_specs=specs,
                out_specs=(rhs_own, rhs_peer),
                scratch_shapes=[
                    weight_scratch,
                    state_scratch,
                    pltpu.VMEM((group, (near_count + 1) * 2 * half, rows), rhs.dtype),
                ],
            ),
            input_output_aliases=aliases,
            compiler_params=params,
        )
        product, send = far(*operands)
        at = others[s] * (chunk * rows)
        most = chunk * rows if s < steps - 1 else chunk * rows * 3 // 4
        for a, b in ((0, most), (most, chunk * rows)):
            if a < b:
                returned.append((swap(send[a:b]), at, a, b))

    row_box = jnp.concatenate([t + jnp.arange(REACH, dtype=jnp.int32) for t in take])
    edge_box = jnp.repeat(jnp.array([(i + 1) * chunk for i in edges], jnp.int32), REACH)
    below = jnp.repeat(jnp.stack(owns), REACH)
    read_box = row_box + jnp.concatenate(
        [lax.dynamic_slice_in_dim(near_offsets, t, REACH, 0) for t in take]
    ).T
    reads = jnp.where(below, read_box < edge_box, read_box >= edge_box)
    meta = jnp.concatenate(
        [h[None].astype(jnp.int32), row_box, jnp.where(reads, read_box, edge_box).reshape(-1),
         reads.astype(jnp.int32).reshape(-1)]
    )
    count = len(edges) * REACH

    def read_spec(k):
        return pl.BlockSpec((rows, columns), lambda j, m: (m[1 + (k + 1) * count + j], 0))

    at_edges = pl.pallas_call(
        edge_kernel,
        out_shape=jax.ShapeDtypeStruct((count * rows, columns), jnp.float32),
        grid_spec=pltpu.PrefetchScalarGridSpec(
            num_scalar_prefetch=1,
            grid=(count,),
            in_specs=[
                pl.BlockSpec((1, near_count, half, rows), lambda j, m: (m[1 + j], 0, 0, 0)),
                pl.BlockSpec((1, near_count, half, rows), lambda j, m: (j, 0, 0, 0)),
                *[read_spec(k) for k in range(near_count)],
            ],
            out_specs=pl.BlockSpec((rows, columns), lambda j, m: (j, 0)),
        ),
        compiler_params=params,
        name="edge_products",
    )(meta, near_t, received["edges"], *[rhs] * near_count)
    added = []
    for s in range(steps):
        products = cut(at_edges, others[s] >> 1, reach_rows)
        place = jnp.where(others[s] & 1, 0, (chunk - REACH) * rows)
        added.append(
            lax.dynamic_update_slice_in_dim(
                jnp.zeros((chunk * rows, columns), jnp.float32), products, place, 0
            )
        )
    for s, (part, at, a, b) in zip([*range(steps), steps - 1], returned):
        part = (part.astype(jnp.float32) + added[s][a:b]).astype(rhs.dtype)
        product = lax.dynamic_update_slice_in_dim(product, part, at + a, 0)
    return product


def solution(mesh):
    placed = (
        P("leaf", "rhs"),
        P("leaf", None, "rhs"),
        P("leaf", None, "rhs"),
        P("leaf", None, None, "rhs"),
        P("leaf", None),
        P(None, "leaf", None, None, "rhs", None),
        P(None, "leaf", None, None, None),
        P(None, "leaf", None, None, "rhs", None),
        P(None, "leaf", None, None, None),
    )
    return jax.shard_map(
        on_device, mesh=mesh, in_specs=placed, out_specs=P("leaf", "rhs"), check_vma=False
    )
```

```python
import functools

import jax
import jax.numpy as jnp
from jax import lax
from jax.experimental import pallas as pl
from jax.experimental.pallas import tpu as pltpu
from jax.sharding import PartitionSpec as P

REACH = 2
SWAP = [(0, 1), (1, 0)]


def parity(value):
    return bin(value).count("1") & 1


def fill_level(weights, own, peer, scales, level, pairs, half, low, high):
    width = scales.shape[-1]
    for p in range(pairs):
        for o in range(2):
            for c in range(2):
                scale = scales[level, p, o, c : c + 1, :]
                for part, at in ((own, low), (peer, high)):
                    block = (part[level, p, o, c].astype(jnp.float32) * scale).astype(jnp.bfloat16)
                    start = pl.multiple_of(o * 2 * half + at, half)
                    weights[p, pl.ds(start, half), c * width : (c + 1) * width] = block


def mix_level(weights, read, write, level, pairs, rank):
    step = 2**level
    for p in range(pairs):
        i = (p >> level) * 2 * step + (p & (step - 1))
        j = i + step
        both = jnp.concatenate([read(i), read(j)], axis=0)
        mixed = jnp.dot(weights[p], both, preferred_element_type=jnp.float32).astype(jnp.bfloat16)
        write(i, mixed[:rank])
        write(j, mixed[rank:])


def source_kernel(idx, rhs_own, rhs_peer, basis_own, basis_peer, own, peer, scales, out, weights, state):
    boxes, rank, _ = out.shape
    rows = basis_own.shape[2]
    half = basis_own.shape[1]
    levels = own.shape[0]
    pairs = boxes // 2
    low = idx[1] * half
    high = (1 - idx[1]) * half
    for b in range(boxes):
        here = pl.ds(b * rows, rows)
        box = jnp.concatenate([rhs_own[here, :], rhs_peer[here, :]], axis=1)
        for part, at in ((basis_own, low), (basis_peer, high)):
            start = pl.multiple_of(b * rank + at, half)
            state[pl.ds(start, half), :] = jnp.dot(
                part[b], box, preferred_element_type=jnp.float32
            ).astype(jnp.bfloat16)

    def read(i):
        return state[i * rank : (i + 1) * rank, :]

    def write_state(i, value):
        state[i * rank : (i + 1) * rank, :] = value

    def write_out(i, value):
        out[i] = value

    for level in range(levels):
        fill_level(weights, own, peer, scales, level, pairs, half, low, high)
        mix_level(weights, read, write_out if level == levels - 1 else write_state, level, pairs, rank)


def target_kernel(
    idx, offsets, mixed, own, peer, scales, basis_own, basis_peer, near_own, near_peer, win_own, win_peer,
    *rest, first,
):
    prod, send, weights, state, left = rest if first else rest[1:]
    boxes, rank, _ = mixed.shape
    half = basis_own.shape[1]
    rows = basis_own.shape[2]
    near_count = near_own.shape[1]
    levels = own.shape[0]
    pairs = boxes // 2
    columns = prod.shape[1]
    low = idx[1] * half
    high = (1 - idx[1]) * half
    step = pl.program_id(0)

    def read_in(i):
        return mixed[i]

    def read_state(i):
        return state[i * rank : (i + 1) * rank, :]

    def write_state(i, value):
        state[i * rank : (i + 1) * rank, :] = value

    for level in range(levels):
        fill_level(weights, own, peer, scales, level, pairs, half, low, high)
        mix_level(weights, read_state if level else read_in, write_state, level, pairs, rank)
    first_box = idx[0] * boxes * pl.num_programs(0) + step * boxes
    for b in range(boxes):
        parts = [read_state(b)]
        for k in range(near_count):
            at = (step * boxes + b + REACH + offsets[(first_box + b) * near_count + k]) * rows
            there = pl.ds(pl.multiple_of(at, rows), rows)
            parts.append(jnp.concatenate([win_own[there, :], win_peer[there, :]], axis=1))
        for k in range(near_count + 1):
            for basis, near, at in ((basis_own, near_own, low), (basis_peer, near_peer, high)):
                start = pl.multiple_of(k * 2 * half + at, half)
                left[b, pl.ds(start, half), :] = near[b, k - 1] if k else basis[b]
        right = jnp.concatenate(parts, axis=0)
        total = lax.dot_general(
            left[b], right, (((0,), (0,)), ((), ())), preferred_element_type=jnp.float32
        ).astype(jnp.bfloat16)
        here = pl.ds(b * rows, rows)
        prod[here, :] = total[:, :columns]
        send[here, :] = total[:, columns:]


def cut_kernel(array, out, sem, *, span, masks):
    at = (lax.axis_index("leaf") // span) ^ jnp.where(lax.axis_index("rhs") == 0, masks[1], masks[0])
    copy = pltpu.make_async_copy(array.at[pl.ds(at * out.shape[0], out.shape[0])], out, sem)
    copy.start()
    copy.wait()


def on_device(
    rhs,
    source_basis,
    target_basis,
    near_blocks,
    near_offsets,
    source_values,
    source_scales,
    target_values,
    target_scales,
):
    leafs = lax.axis_size("leaf")
    box_count, rows, half = source_basis.shape
    columns = rhs.shape[1]
    levels = source_values.shape[0]
    rank = source_values.shape[5]
    near_count = near_blocks.shape[1]
    group = 2**levels
    chunk = 2 * group
    chunks = box_count // chunk
    quota = box_count // leafs
    span = chunk // quota
    bits = span.bit_length() - 1
    steps = chunks // 2
    masks = [[m for m in range(chunks - 1, -1, -1) if parity(m) == h] for h in range(2)]

    d = lax.axis_index("leaf")
    h = lax.axis_index("rhs")
    home = d >> bits
    mine = [home ^ jnp.where(h == 0, masks[0][s], masks[1][s]) for s in range(steps)]
    others = [home ^ jnp.where(h == 0, masks[1][s], masks[0][s]) for s in range(steps)]
    home_parity = sum(((home >> k) & 1) for k in range(chunks.bit_length())) & 1

    source_t = jnp.swapaxes(source_basis, 1, 2)
    target_t = jnp.swapaxes(target_basis, 1, 2)
    near_t = jnp.swapaxes(near_blocks, 2, 3)

    def cut(array, at, size, axis=0):
        return lax.dynamic_slice_in_dim(array, at * size, size, axis)

    def swap(array):
        return lax.ppermute(array, "rhs", SWAP)

    edges = [i for i in range(chunks - 1) if parity(i) != parity(i + 1)]
    assert edges == list(range(0, chunks, 2))
    owns = [(home_parity ^ parity(i)) == h for i in edges]
    edge_pairs = [(i, j) for i in range(REACH) for j in range(REACH - i)]
    reach_rows = REACH * rows

    def edge_sums(near, mine_too):
        sums = []
        for i, own in zip(edges, owns):
            left = own if mine_too else ~own
            at = (i + 1) * chunk - jnp.where(left, REACH, 0)
            blocks = lax.dynamic_slice_in_dim(near, at, REACH, 0).astype(jnp.float32)
            offset = lax.dynamic_slice_in_dim(near_offsets, at, REACH, 0)
            blocks = jnp.where(left, blocks[::-1], blocks)
            offset = jnp.where(left, -offset[::-1], offset)
            for row, source in edge_pairs:
                reads = (offset[row] == -(row + source + 1))[:, None, None]
                sums.append(jnp.sum(jnp.where(reads, blocks[row], 0.0), axis=0).astype(near.dtype))
        return jnp.stack(sums)

    half_pairs = chunk // 2
    pool = {
        "rhs": (rhs, chunk * rows, 0),
        "source": (source_t, chunk, 0),
        "source_blocks": (source_values, half_pairs, 1),
        "target": (target_t, chunk, 0),
        "target_blocks": (target_values, half_pairs, 1),
        "near": (near_t, chunk, 0),
    }
    arrays = {name: entry[0] for name, entry in pool.items()}
    queue = [(name, s) for s in range(steps) for name in ("source", "rhs", "source_blocks")]
    for s in range(steps):
        queue += [(name, s) for name in ("target_blocks", "target", "near")]
    queue += ["edges"]
    first_cut = pl.pallas_call(
        functools.partial(cut_kernel, span=span, masks=[masks[0][0], masks[1][0]]),
        out_shape=pltpu.VMEM((chunk, half, rows), rhs.dtype),
        in_specs=[pl.BlockSpec(memory_space=pl.ANY)],
        out_specs=pl.BlockSpec(memory_space=pltpu.VMEM),
        scratch_shapes=[pltpu.SemaphoreType.DMA],
        name="first_cut",
    )
    received = {}
    for n, entry in enumerate(queue):
        if entry == "edges":
            piece = edge_sums(arrays["near"], True)
        else:
            name, s = entry
            piece = cut(arrays[name], others[s], pool[name][1], pool[name][2]) if n else first_cut(arrays[name])
        piece, arrays = lax.optimization_barrier((piece, arrays))
        received[entry] = swap(piece)

    peer_rhs = jnp.zeros(((box_count + 2 * REACH) * rows, columns), rhs.dtype)
    for s in range(steps):
        peer_rhs = lax.dynamic_update_slice_in_dim(
            peer_rhs, received["rhs", s], mine[s] * (chunk * rows) + reach_rows, 0
        )
    peer_tail = peer_rhs[box_count * rows : box_count * rows + reach_rows]
    peer_head = peer_rhs[reach_rows : 2 * reach_rows]
    up = [(i, i + 1) for i in range(leafs - 1)]
    down = [(i + 1, i) for i in range(leafs - 1)]
    tail = rhs[-reach_rows:]
    head = rhs[:reach_rows]

    def side(device):
        return parity(device >> bits)

    def same_side(other):
        return (sum((((other >> bits) >> k) & 1) for k in range(chunks.bit_length())) & 1) == home_parity

    both = ("leaf", "rhs")
    low_peer = lax.ppermute(
        jnp.where(same_side(d + 1), peer_tail, tail), both,
        [(2 * a + side(a), 2 * b + side(b)) for a, b in up],
    )
    high_peer = lax.ppermute(
        jnp.where(same_side(d - 1), peer_head, head), both,
        [(2 * a + side(a), 2 * b + side(b)) for a, b in down],
    )
    peer_rhs = lax.dynamic_update_slice_in_dim(peer_rhs, low_peer, 0, 0)
    peer_rhs = lax.dynamic_update_slice_in_dim(peer_rhs, high_peer, box_count * rows + reach_rows, 0)
    own_rhs = jnp.concatenate(
        [lax.ppermute(tail, "leaf", up), rhs, lax.ppermute(head, "leaf", down)], axis=0
    )

    params = pltpu.CompilerParams(
        dimension_semantics=("arbitrary",), vmem_limit_bytes=56 * 2**20
    )
    pair_count = group // 2
    wide = 2 * columns
    blocks_own = pl.BlockSpec(
        (levels, pair_count, 2, 2, half, rank), lambda t, i, *_: (0, i[0] * 2 + t, 0, 0, 0, 0)
    )
    blocks_peer = pl.BlockSpec((levels, pair_count, 2, 2, half, rank), lambda t, *_: (0, t, 0, 0, 0, 0))
    scale_spec = pl.BlockSpec(
        (levels, pair_count, 2, 2, rank), lambda t, i, *_: (0, i[0] * 2 + t, 0, 0, 0)
    )
    basis_own = pl.BlockSpec((group, half, rows), lambda t, i, *_: (i[0] * 2 + t, 0, 0))
    basis_peer = pl.BlockSpec((group, half, rows), lambda t, *_: (t, 0, 0))
    near_own = pl.BlockSpec((group, near_count, half, rows), lambda t, i, *_: (i[0] * 2 + t, 0, 0, 0))
    near_peer = pl.BlockSpec((group, near_count, half, rows), lambda t, *_: (t, 0, 0, 0))
    state_spec = pl.BlockSpec((group, rank, wide), lambda t, *_: (t, 0, 0))
    rhs_own = pl.BlockSpec((group * rows, columns), lambda t, i, *_: (i[0] * 2 + t, 0))
    rhs_peer = pl.BlockSpec((group * rows, columns), lambda t, *_: (t, 0))
    window_rows = (chunk + 2 * REACH) * rows
    window = pl.BlockSpec((window_rows, columns), lambda t, *_: (0, 0))
    weight_scratch = pltpu.VMEM((pair_count, 2 * rank, 2 * rank), rhs.dtype)
    state_scratch = pltpu.VMEM((group * rank, wide), rhs.dtype)

    rows_in = []
    for s in range(steps):
        index = jnp.stack([mine[s], h]).astype(jnp.int32)
        mixed = pl.pallas_call(
            source_kernel,
            out_shape=jax.ShapeDtypeStruct((chunk, rank, wide), rhs.dtype),
            grid_spec=pltpu.PrefetchScalarGridSpec(
                num_scalar_prefetch=1,
                grid=(2,),
                in_specs=[rhs_own, rhs_peer, basis_own, basis_peer, blocks_own, blocks_peer, scale_spec],
                out_specs=state_spec,
                scratch_shapes=[weight_scratch, state_scratch],
            ),
            compiler_params=params,
        )(index, rhs, received["rhs", s], source_t, received["source", s], source_values, received["source_blocks", s], source_scales)
        arrived = jnp.zeros((chunk, rank, wide), rhs.dtype)
        for k in range(span):
            slot = (d ^ k) & (span - 1)
            pairs = [
                (2 * a + e, 2 * (a ^ ((masks[e][s] << bits) | k)) + e) for a in range(leafs) for e in range(2)
            ]
            piece = lax.ppermute(cut(mixed, slot, quota), both, pairs)
            arrived = lax.dynamic_update_slice_in_dim(arrived, piece, slot * quota, 0)
        rows_in.append(arrived)

    offsets = near_offsets.reshape(-1)
    product = None
    returned = []
    for s in range(steps):
        index = jnp.stack([mine[s], h]).astype(jnp.int32)
        start = mine[s] * (chunk * rows)
        operands = [
            index, offsets, rows_in[s], target_values, received["target_blocks", s], target_scales,
            target_t, received["target", s], near_t, received["near", s],
            lax.dynamic_slice_in_dim(own_rhs, start, window_rows, 0),
            lax.dynamic_slice_in_dim(peer_rhs, start, window_rows, 0),
        ]
        specs = [
            state_spec, blocks_own, blocks_peer, scale_spec, basis_own, basis_peer, near_own, near_peer,
            window, window,
        ]
        aliases = {}
        if s:
            aliases = {len(operands): 0}
            operands.append(product)
            specs.append(pl.BlockSpec(memory_space=pl.ANY))
        far = pl.pallas_call(
            functools.partial(target_kernel, first=s == 0),
            out_shape=(
                jax.ShapeDtypeStruct((box_count * rows, columns), rhs.dtype),
                jax.ShapeDtypeStruct((chunk * rows, columns), rhs.dtype),
            ),
            grid_spec=pltpu.PrefetchScalarGridSpec(
                num_scalar_prefetch=2,
                grid=(2,),
                in_specs=specs,
                out_specs=(rhs_own, rhs_peer),
                scratch_shapes=[
                    weight_scratch,
                    state_scratch,
                    pltpu.VMEM((group, (near_count + 1) * 2 * half, rows), rhs.dtype),
                ],
            ),
            input_output_aliases=aliases,
            compiler_params=params,
        )
        product, send = far(*operands)
        at = others[s] * (chunk * rows)
        most = chunk * rows if s < steps - 1 else chunk * rows * 7 // 8
        for a, b in ((0, most), (most, chunk * rows)):
            if a < b:
                returned.append((swap(send[a:b]), at, a, b))

    own_sums, peer_sums = edge_sums(near_t, False), received["edges"]
    sums = jnp.where(
        h == 0,
        jnp.concatenate([own_sums, peer_sums], axis=1),
        jnp.concatenate([peer_sums, own_sums], axis=1),
    )
    at_edges = []
    for n, (i, own) in enumerate(zip(edges, owns)):
        sources = lax.dynamic_slice_in_dim(rhs, ((i + 1) * chunk - jnp.where(own, REACH, 0)) * rows, reach_rows, 0)
        sources = sources.reshape(REACH, rows, columns)
        sources = jnp.where(own, sources[::-1], sources)
        products = [jnp.zeros((rows, columns), jnp.float32) for _ in range(REACH)]
        for p, (row, source) in enumerate(edge_pairs):
            products[row] += lax.dot_general(
                sums[n * len(edge_pairs) + p], sources[source], (((0,), (0,)), ((), ())),
                preferred_element_type=jnp.float32,
            )
        products = jnp.stack(products)
        at_edges.append(jnp.where(own, products, products[::-1]).reshape(reach_rows, columns))
    at_edges = jnp.concatenate(at_edges, axis=0)
    added = []
    for s in range(steps):
        products = cut(at_edges, others[s] >> 1, reach_rows)
        place = jnp.where(others[s] & 1, 0, (chunk - REACH) * rows)
        added.append(
            lax.dynamic_update_slice_in_dim(
                jnp.zeros((chunk * rows, columns), jnp.float32), products, place, 0
            )
        )
    for s, (part, at, a, b) in zip([*range(steps), steps - 1], returned):
        part = (part.astype(jnp.float32) + added[s][a:b]).astype(rhs.dtype)
        product = lax.dynamic_update_slice_in_dim(product, part, at + a, 0)
    return product


def solution(mesh):
    placed = (
        P("leaf", "rhs"),
        P("leaf", None, "rhs"),
        P("leaf", None, "rhs"),
        P("leaf", None, None, "rhs"),
        P("leaf", None),
        P(None, "leaf", None, None, "rhs", None),
        P(None, "leaf", None, None, None),
        P(None, "leaf", None, None, "rhs", None),
        P(None, "leaf", None, None, None),
    )
    return jax.shard_map(
        on_device, mesh=mesh, in_specs=placed, out_specs=P("leaf", "rhs"), check_vma=False
    )
```

```python
import functools

import jax
import jax.numpy as jnp
from jax import lax
from jax.experimental import pallas as pl
from jax.experimental.pallas import tpu as pltpu
from jax.sharding import PartitionSpec as P

REACH = 2
SWAP = [(0, 1), (1, 0)]


def parity(value):
    return bin(value).count("1") & 1


def fill_level(weights, own, peer, scales, level, pairs, half, low, high):
    width = scales.shape[-1]
    for p in range(pairs):
        for o in range(2):
            for c in range(2):
                scale = scales[level, p, o, c : c + 1, :]
                for part, at in ((own, low), (peer, high)):
                    block = (part[level, p, o, c].astype(jnp.float32) * scale).astype(jnp.bfloat16)
                    start = pl.multiple_of(o * 2 * half + at, half)
                    weights[p, pl.ds(start, half), c * width : (c + 1) * width] = block


def mix_level(weights, read, write, level, pairs, rank):
    step = 2**level
    for p in range(pairs):
        i = (p >> level) * 2 * step + (p & (step - 1))
        j = i + step
        both = jnp.concatenate([read(i), read(j)], axis=0)
        mixed = jnp.dot(weights[p], both, preferred_element_type=jnp.float32).astype(jnp.bfloat16)
        write(i, mixed[:rank])
        write(j, mixed[rank:])


def source_kernel(idx, rhs_own, rhs_peer, basis_own, basis_peer, own, peer, scales, out, weights, state):
    boxes, rank, _ = out.shape
    rows = basis_own.shape[2]
    half = basis_own.shape[1]
    levels = own.shape[0]
    pairs = boxes // 2
    low = idx[1] * half
    high = (1 - idx[1]) * half
    for b in range(boxes):
        here = pl.ds(b * rows, rows)
        box = jnp.concatenate([rhs_own[here, :], rhs_peer[here, :]], axis=1)
        for part, at in ((basis_own, low), (basis_peer, high)):
            start = pl.multiple_of(b * rank + at, half)
            state[pl.ds(start, half), :] = jnp.dot(
                part[b], box, preferred_element_type=jnp.float32
            ).astype(jnp.bfloat16)

    def read(i):
        return state[i * rank : (i + 1) * rank, :]

    def write_state(i, value):
        state[i * rank : (i + 1) * rank, :] = value

    def write_out(i, value):
        out[i] = value

    for level in range(levels):
        fill_level(weights, own, peer, scales, level, pairs, half, low, high)
        mix_level(weights, read, write_out if level == levels - 1 else write_state, level, pairs, rank)


def target_kernel(
    idx, offsets, mixed, own, peer, scales, basis_own, basis_peer, near_own, near_peer, win_own, win_peer,
    *rest, first,
):
    prod, send, weights, state, left = rest if first else rest[1:]
    boxes, rank, _ = mixed.shape
    half = basis_own.shape[1]
    rows = basis_own.shape[2]
    near_count = near_own.shape[1]
    levels = own.shape[0]
    pairs = boxes // 2
    columns = prod.shape[1]
    low = idx[1] * half
    high = (1 - idx[1]) * half
    step = pl.program_id(0)

    def read_in(i):
        return mixed[i]

    def read_state(i):
        return state[i * rank : (i + 1) * rank, :]

    def write_state(i, value):
        state[i * rank : (i + 1) * rank, :] = value

    for level in range(levels):
        fill_level(weights, own, peer, scales, level, pairs, half, low, high)
        mix_level(weights, read_state if level else read_in, write_state, level, pairs, rank)
    first_box = idx[0] * boxes * pl.num_programs(0) + step * boxes
    for b in range(boxes):
        parts = [read_state(b)]
        for k in range(near_count):
            at = (step * boxes + b + REACH + offsets[(first_box + b) * near_count + k]) * rows
            there = pl.ds(pl.multiple_of(at, rows), rows)
            parts.append(jnp.concatenate([win_own[there, :], win_peer[there, :]], axis=1))
        for k in range(near_count + 1):
            for basis, near, at in ((basis_own, near_own, low), (basis_peer, near_peer, high)):
                start = pl.multiple_of(k * 2 * half + at, half)
                left[b, pl.ds(start, half), :] = near[b, k - 1] if k else basis[b]
        right = jnp.concatenate(parts, axis=0)
        total = lax.dot_general(
            left[b], right, (((0,), (0,)), ((), ())), preferred_element_type=jnp.float32
        ).astype(jnp.bfloat16)
        here = pl.ds(b * rows, rows)
        prod[here, :] = total[:, :columns]
        send[here, :] = total[:, columns:]


def cut_kernel(array, out, sem, *, span, masks):
    at = (lax.axis_index("leaf") // span) ^ jnp.where(lax.axis_index("rhs") == 0, masks[1], masks[0])
    copy = pltpu.make_async_copy(array.at[pl.ds(at * out.shape[0], out.shape[0])], out, sem)
    copy.start()
    copy.wait()


def on_device(
    rhs,
    source_basis,
    target_basis,
    near_blocks,
    near_offsets,
    source_values,
    source_scales,
    target_values,
    target_scales,
):
    leafs = lax.axis_size("leaf")
    box_count, rows, half = source_basis.shape
    columns = rhs.shape[1]
    levels = source_values.shape[0]
    rank = source_values.shape[5]
    near_count = near_blocks.shape[1]
    group = 2**levels
    chunk = 2 * group
    chunks = box_count // chunk
    quota = box_count // leafs
    span = chunk // quota
    bits = span.bit_length() - 1
    steps = chunks // 2
    masks = [[m for m in range(chunks - 1, -1, -1) if parity(m) == h] for h in range(2)]

    d = lax.axis_index("leaf")
    h = lax.axis_index("rhs")
    home = d >> bits
    mine = [home ^ jnp.where(h == 0, masks[0][s], masks[1][s]) for s in range(steps)]
    others = [home ^ jnp.where(h == 0, masks[1][s], masks[0][s]) for s in range(steps)]
    home_parity = sum(((home >> k) & 1) for k in range(chunks.bit_length())) & 1

    source_t = jnp.swapaxes(source_basis, 1, 2)
    target_t = jnp.swapaxes(target_basis, 1, 2)
    near_t = jnp.swapaxes(near_blocks, 2, 3)

    def cut(array, at, size, axis=0):
        return lax.dynamic_slice_in_dim(array, at * size, size, axis)

    def swap(array):
        return lax.ppermute(array, "rhs", SWAP)

    edges = [i for i in range(chunks - 1) if parity(i) != parity(i + 1)]
    assert edges == list(range(0, chunks, 2))
    owns = [(home_parity ^ parity(i)) == h for i in edges]
    edge_pairs = [(i, j) for i in range(REACH) for j in range(REACH - i)]
    reach_rows = REACH * rows

    def row_sums(near, at, left):
        blocks = lax.dynamic_slice_in_dim(near, at, REACH, 0).astype(jnp.float32)
        offset = lax.dynamic_slice_in_dim(near_offsets, at, REACH, 0)
        blocks = jnp.where(left, blocks[::-1], blocks)
        offset = jnp.where(left, -offset[::-1], offset)
        sums = []
        for row, source in edge_pairs:
            reads = (offset[row] == -(row + source + 1))[:, None, None]
            sums.append(jnp.sum(jnp.where(reads, blocks[row], 0.0), axis=0).astype(near.dtype))
        return sums

    def edge_sums(near, mine_too):
        sums = []
        for i, own in zip(edges, owns):
            left = own if mine_too else ~own
            sums += row_sums(near, (i + 1) * chunk - jnp.where(left, REACH, 0), left)
        return jnp.stack(sums)

    def side(device):
        return parity(device >> bits)

    def moved(other):
        other_parity = sum((((other >> bits) >> k) & 1) for k in range(chunks.bit_length())) & 1
        return (other >= 0) & (other < leafs) & (other_parity != home_parity)

    assert span > 1
    low_moved, high_moved = moved(d - 1), moved(d + 1)
    ends = [(a, a + 1) for a in range(leafs - 1) if side(a) != side(a + 1)]
    end_pairs = [(2 * a + side(a), 2 * a + 1 - side(a)) for pair in ends for a in pair]
    end_rows = jnp.where(high_moved, box_count - REACH, 0)

    half_pairs = chunk // 2
    pool = {
        "rhs": (rhs, chunk * rows, 0),
        "source": (source_t, chunk, 0),
        "source_blocks": (source_values, half_pairs, 1),
        "target": (target_t, chunk, 0),
        "target_blocks": (target_values, half_pairs, 1),
        "near": (near_t, chunk, 0),
    }
    arrays = {name: entry[0] for name, entry in pool.items()}
    queue = [(name, s) for s in range(steps) for name in ("source", "rhs", "source_blocks")]
    for s in range(steps):
        queue += [(name, s) for name in ("target_blocks", "target", "near")]
    queue += ["edges", "ends"]
    first_cut = pl.pallas_call(
        functools.partial(cut_kernel, span=span, masks=[masks[0][0], masks[1][0]]),
        out_shape=pltpu.VMEM((chunk, half, rows), rhs.dtype),
        in_specs=[pl.BlockSpec(memory_space=pl.ANY)],
        out_specs=pl.BlockSpec(memory_space=pltpu.VMEM),
        scratch_shapes=[pltpu.SemaphoreType.DMA],
        name="first_cut",
    )
    both = ("leaf", "rhs")
    received = {}
    for n, entry in enumerate(queue):
        if entry == "edges":
            piece = edge_sums(arrays["near"], True)
        elif entry == "ends":
            piece = jnp.stack(row_sums(arrays["near"], end_rows, high_moved))
        else:
            name, s = entry
            piece = cut(arrays[name], others[s], pool[name][1], pool[name][2]) if n else first_cut(arrays[name])
        piece, arrays = lax.optimization_barrier((piece, arrays))
        received[entry] = lax.ppermute(piece, both, end_pairs) if entry == "ends" else swap(piece)

    peer_rhs = jnp.zeros(((box_count + 2 * REACH) * rows, columns), rhs.dtype)
    for s in range(steps):
        peer_rhs = lax.dynamic_update_slice_in_dim(
            peer_rhs, received["rhs", s], mine[s] * (chunk * rows) + reach_rows, 0
        )
    peer_tail = peer_rhs[box_count * rows : box_count * rows + reach_rows]
    peer_head = peer_rhs[reach_rows : 2 * reach_rows]
    up = [(i, i + 1) for i in range(leafs - 1)]
    down = [(i + 1, i) for i in range(leafs - 1)]
    ends_in = []
    for rows_out, way in ((arrays["rhs"][-reach_rows:], up), (arrays["rhs"][:reach_rows], down)):
        ends_in.append(lax.ppermute(rows_out, "leaf", way))
    for rows_out, way in ((peer_tail, up), (peer_head, down)):
        pairs = [(2 * a + side(a), 2 * b + side(b)) for a, b in way if side(a) == side(b)]
        ends_in.append(lax.ppermute(rows_out, both, pairs))
    low_own, high_own, low_peer, high_peer = ends_in
    peer_rhs = lax.dynamic_update_slice_in_dim(peer_rhs, low_peer, 0, 0)
    peer_rhs = lax.dynamic_update_slice_in_dim(peer_rhs, high_peer, box_count * rows + reach_rows, 0)
    own_rhs = jnp.concatenate([low_own, rhs, high_own], axis=0)

    params = pltpu.CompilerParams(
        dimension_semantics=("arbitrary",), vmem_limit_bytes=56 * 2**20
    )
    pair_count = group // 2
    wide = 2 * columns
    blocks_own = pl.BlockSpec(
        (levels, pair_count, 2, 2, half, rank), lambda t, i, *_: (0, i[0] * 2 + t, 0, 0, 0, 0)
    )
    blocks_peer = pl.BlockSpec((levels, pair_count, 2, 2, half, rank), lambda t, *_: (0, t, 0, 0, 0, 0))
    scale_spec = pl.BlockSpec(
        (levels, pair_count, 2, 2, rank), lambda t, i, *_: (0, i[0] * 2 + t, 0, 0, 0)
    )
    basis_own = pl.BlockSpec((group, half, rows), lambda t, i, *_: (i[0] * 2 + t, 0, 0))
    basis_peer = pl.BlockSpec((group, half, rows), lambda t, *_: (t, 0, 0))
    near_own = pl.BlockSpec((group, near_count, half, rows), lambda t, i, *_: (i[0] * 2 + t, 0, 0, 0))
    near_peer = pl.BlockSpec((group, near_count, half, rows), lambda t, *_: (t, 0, 0, 0))
    state_spec = pl.BlockSpec((group, rank, wide), lambda t, *_: (t, 0, 0))
    rhs_own = pl.BlockSpec((group * rows, columns), lambda t, i, *_: (i[0] * 2 + t, 0))
    rhs_peer = pl.BlockSpec((group * rows, columns), lambda t, *_: (t, 0))
    window_rows = (chunk + 2 * REACH) * rows
    window = pl.BlockSpec((window_rows, columns), lambda t, *_: (0, 0))
    weight_scratch = pltpu.VMEM((pair_count, 2 * rank, 2 * rank), rhs.dtype)
    state_scratch = pltpu.VMEM((group * rank, wide), rhs.dtype)

    rows_in = []
    for s in range(steps):
        index = jnp.stack([mine[s], h]).astype(jnp.int32)
        mixed = pl.pallas_call(
            source_kernel,
            out_shape=jax.ShapeDtypeStruct((chunk, rank, wide), rhs.dtype),
            grid_spec=pltpu.PrefetchScalarGridSpec(
                num_scalar_prefetch=1,
                grid=(2,),
                in_specs=[rhs_own, rhs_peer, basis_own, basis_peer, blocks_own, blocks_peer, scale_spec],
                out_specs=state_spec,
                scratch_shapes=[weight_scratch, state_scratch],
            ),
            compiler_params=params,
        )(index, rhs, received["rhs", s], source_t, received["source", s], source_values, received["source_blocks", s], source_scales)
        arrived = jnp.zeros((chunk, rank, wide), rhs.dtype)
        for k in range(span):
            slot = (d ^ k) & (span - 1)
            pairs = [
                (2 * a + e, 2 * (a ^ ((masks[e][s] << bits) | k)) + e) for a in range(leafs) for e in range(2)
            ]
            piece = lax.ppermute(cut(mixed, slot, quota), both, pairs)
            arrived = lax.dynamic_update_slice_in_dim(arrived, piece, slot * quota, 0)
        rows_in.append(arrived)

    offsets = near_offsets.reshape(-1)
    product = None
    returned = []
    for s in range(steps):
        index = jnp.stack([mine[s], h]).astype(jnp.int32)
        start = mine[s] * (chunk * rows)
        operands = [
            index, offsets, rows_in[s], target_values, received["target_blocks", s], target_scales,
            target_t, received["target", s], near_t, received["near", s],
            lax.dynamic_slice_in_dim(own_rhs, start, window_rows, 0),
            lax.dynamic_slice_in_dim(peer_rhs, start, window_rows, 0),
        ]
        specs = [
            state_spec, blocks_own, blocks_peer, scale_spec, basis_own, basis_peer, near_own, near_peer,
            window, window,
        ]
        aliases = {}
        if s:
            aliases = {len(operands): 0}
            operands.append(product)
            specs.append(pl.BlockSpec(memory_space=pl.ANY))
        far = pl.pallas_call(
            functools.partial(target_kernel, first=s == 0),
            out_shape=(
                jax.ShapeDtypeStruct((box_count * rows, columns), rhs.dtype),
                jax.ShapeDtypeStruct((chunk * rows, columns), rhs.dtype),
            ),
            grid_spec=pltpu.PrefetchScalarGridSpec(
                num_scalar_prefetch=2,
                grid=(2,),
                in_specs=specs,
                out_specs=(rhs_own, rhs_peer),
                scratch_shapes=[
                    weight_scratch,
                    state_scratch,
                    pltpu.VMEM((group, (near_count + 1) * 2 * half, rows), rhs.dtype),
                ],
            ),
            input_output_aliases=aliases,
            compiler_params=params,
        )
        product, send = far(*operands)
        at = others[s] * (chunk * rows)
        size = chunk * rows
        spans = [(0, size)]
        if s == steps - 1:
            middle = size // 2
            spans = [(0, middle - rows), (middle + rows, size), (middle - rows, middle + rows)]
        for a, b in spans:
            returned.append((s, swap(send[a:b]), at, a, b))

    own_sums = [edge_sums(near_t, False), jnp.stack(row_sums(near_t, end_rows, high_moved))]

    def products_of(own, peer, sources, left):
        sums = jnp.where(
            h == 0, jnp.concatenate([own, peer], axis=1), jnp.concatenate([peer, own], axis=1)
        )
        sources = sources.reshape(REACH, rows, columns)
        sources = jnp.where(left, sources[::-1], sources)
        products = [jnp.zeros((rows, columns), jnp.float32) for _ in range(REACH)]
        for p, (row, source) in enumerate(edge_pairs):
            products[row] += lax.dot_general(
                sums[p], sources[source], (((0,), (0,)), ((), ())), preferred_element_type=jnp.float32
            )
        products = jnp.stack(products)
        return jnp.where(left, products, products[::-1]).reshape(reach_rows, columns)

    count = len(edge_pairs)
    at_edges = []
    for n, (i, own) in enumerate(zip(edges, owns)):
        start = (i + 1) * chunk - jnp.where(own, REACH, 0)
        at_edges.append(
            products_of(
                own_sums[0][n * count : (n + 1) * count],
                received["edges"][n * count : (n + 1) * count],
                lax.dynamic_slice_in_dim(arrays["rhs"], start * rows, reach_rows, 0),
                own,
            )
        )
    at_edges = jnp.concatenate(at_edges, axis=0)
    at_end = products_of(
        own_sums[1], received["ends"], jnp.where(high_moved, high_own, low_own), ~high_moved
    )
    at_end = jnp.where((low_moved | high_moved) & (home_parity != h), at_end, 0.0)
    added = []
    for s in range(steps):
        inner = cut(at_edges, others[s] >> 1, reach_rows)
        first = jnp.where(others[s] & 1, inner, jnp.where((others[s] == 0) & ~high_moved, at_end, 0.0))
        last = jnp.where(others[s] & 1, jnp.where((others[s] == chunks - 1) & high_moved, at_end, 0.0), inner)
        middle = jnp.zeros(((chunk - 2 * REACH) * rows, columns), jnp.float32)
        added.append(jnp.concatenate([first, middle, last], axis=0))
    added = lax.optimization_barrier(added)
    for s, part, at, a, b in returned:
        if a < reach_rows or b > chunk * rows - reach_rows:
            part = (part.astype(jnp.float32) + added[s][a:b]).astype(rhs.dtype)
        product = lax.dynamic_update_slice_in_dim(product, part, at + a, 0)
    return product


def solution(mesh):
    placed = (
        P("leaf", "rhs"),
        P("leaf", None, "rhs"),
        P("leaf", None, "rhs"),
        P("leaf", None, None, "rhs"),
        P("leaf", None),
        P(None, "leaf", None, None, "rhs", None),
        P(None, "leaf", None, None, None),
        P(None, "leaf", None, None, "rhs", None),
        P(None, "leaf", None, None, None),
    )
    return jax.shard_map(
        on_device, mesh=mesh, in_specs=placed, out_specs=P("leaf", "rhs"), check_vma=False
    )
```

```python
import functools

import jax
import jax.numpy as jnp
from jax import lax
from jax.experimental import pallas as pl
from jax.experimental.pallas import tpu as pltpu
from jax.sharding import PartitionSpec as P

REACH = 2
SWAP = [(0, 1), (1, 0)]


def parity(value):
    return bin(value).count("1") & 1


def fill_level(weights, own, peer, scales, level, pairs, half, low, high):
    width = scales.shape[-1]
    for p in range(pairs):
        for o in range(2):
            for c in range(2):
                scale = scales[level, p, o, c : c + 1, :]
                for part, at in ((own, low), (peer, high)):
                    block = (part[level, p, o, c].astype(jnp.float32) * scale).astype(jnp.bfloat16)
                    start = pl.multiple_of(o * 2 * half + at, half)
                    weights[p, pl.ds(start, half), c * width : (c + 1) * width] = block


def mix_level(weights, read, write, level, pairs, rank):
    step = 2**level
    for p in range(pairs):
        i = (p >> level) * 2 * step + (p & (step - 1))
        j = i + step
        both = jnp.concatenate([read(i), read(j)], axis=0)
        mixed = jnp.dot(weights[p], both, preferred_element_type=jnp.float32).astype(jnp.bfloat16)
        write(i, mixed[:rank])
        write(j, mixed[rank:])


def source_kernel(idx, rhs_own, rhs_peer, basis_own, basis_peer, own, peer, scales, out, weights, state):
    boxes, rank, _ = out.shape
    rows = basis_own.shape[2]
    half = basis_own.shape[1]
    levels = own.shape[0]
    pairs = boxes // 2
    low = idx[1] * half
    high = (1 - idx[1]) * half
    for b in range(boxes):
        here = pl.ds(b * rows, rows)
        box = jnp.concatenate([rhs_own[here, :], rhs_peer[here, :]], axis=1)
        for part, at in ((basis_own, low), (basis_peer, high)):
            start = pl.multiple_of(b * rank + at, half)
            state[pl.ds(start, half), :] = jnp.dot(
                part[b], box, preferred_element_type=jnp.float32
            ).astype(jnp.bfloat16)

    def read(i):
        return state[i * rank : (i + 1) * rank, :]

    def write_state(i, value):
        state[i * rank : (i + 1) * rank, :] = value

    def write_out(i, value):
        out[i] = value

    for level in range(levels):
        fill_level(weights, own, peer, scales, level, pairs, half, low, high)
        mix_level(weights, read, write_out if level == levels - 1 else write_state, level, pairs, rank)


def target_kernel(
    idx, offsets, mixed, own, peer, scales, basis_own, basis_peer, near_own, near_peer, win_own, win_peer,
    *rest, first,
):
    prod, send, weights, state, left = rest if first else rest[1:]
    boxes, rank, _ = mixed.shape
    half = basis_own.shape[1]
    rows = basis_own.shape[2]
    near_count = near_own.shape[1]
    levels = own.shape[0]
    pairs = boxes // 2
    columns = prod.shape[1]
    low = idx[1] * half
    high = (1 - idx[1]) * half
    step = pl.program_id(0)

    def read_in(i):
        return mixed[i]

    def read_state(i):
        return state[i * rank : (i + 1) * rank, :]

    def write_state(i, value):
        state[i * rank : (i + 1) * rank, :] = value

    for level in range(levels):
        fill_level(weights, own, peer, scales, level, pairs, half, low, high)
        mix_level(weights, read_state if level else read_in, write_state, level, pairs, rank)
    first_box = idx[0] * boxes * pl.num_programs(0) + step * boxes
    for b in range(boxes):
        parts = [read_state(b)]
        for k in range(near_count):
            at = (step * boxes + b + REACH + offsets[(first_box + b) * near_count + k]) * rows
            there = pl.ds(pl.multiple_of(at, rows), rows)
            parts.append(jnp.concatenate([win_own[there, :], win_peer[there, :]], axis=1))
        for k in range(near_count + 1):
            for basis, near, at in ((basis_own, near_own, low), (basis_peer, near_peer, high)):
                start = pl.multiple_of(k * 2 * half + at, half)
                left[b, pl.ds(start, half), :] = near[b, k - 1] if k else basis[b]
        right = jnp.concatenate(parts, axis=0)
        total = lax.dot_general(
            left[b], right, (((0,), (0,)), ((), ())), preferred_element_type=jnp.float32
        ).astype(jnp.bfloat16)
        here = pl.ds(b * rows, rows)
        prod[here, :] = total[:, :columns]
        send[here, :] = total[:, columns:]


def cut_kernel(array, out, sem, *, span, masks):
    at = (lax.axis_index("leaf") // span) ^ jnp.where(lax.axis_index("rhs") == 0, masks[1], masks[0])
    copy = pltpu.make_async_copy(array.at[pl.ds(at * out.shape[0], out.shape[0])], out, sem)
    copy.start()
    copy.wait()


def on_device(
    rhs,
    source_basis,
    target_basis,
    near_blocks,
    near_offsets,
    source_values,
    source_scales,
    target_values,
    target_scales,
):
    leafs = lax.axis_size("leaf")
    box_count, rows, half = source_basis.shape
    columns = rhs.shape[1]
    levels = source_values.shape[0]
    rank = source_values.shape[5]
    near_count = near_blocks.shape[1]
    group = 2**levels
    chunk = 2 * group
    chunks = box_count // chunk
    quota = box_count // leafs
    span = chunk // quota
    bits = span.bit_length() - 1
    steps = chunks // 2
    masks = [[m for m in range(chunks - 1, -1, -1) if parity(m) == h] for h in range(2)]

    d = lax.axis_index("leaf")
    h = lax.axis_index("rhs")
    home = d >> bits
    mine = [home ^ jnp.where(h == 0, masks[0][s], masks[1][s]) for s in range(steps)]
    others = [home ^ jnp.where(h == 0, masks[1][s], masks[0][s]) for s in range(steps)]
    home_parity = sum(((home >> k) & 1) for k in range(chunks.bit_length())) & 1

    source_t = jnp.swapaxes(source_basis, 1, 2)
    target_t = jnp.swapaxes(target_basis, 1, 2)
    near_t = jnp.swapaxes(near_blocks, 2, 3)

    def cut(array, at, size, axis=0):
        return lax.dynamic_slice_in_dim(array, at * size, size, axis)

    def swap(array):
        return lax.ppermute(array, "rhs", SWAP)

    edges = [i for i in range(chunks - 1) if parity(i) != parity(i + 1)]
    assert edges == list(range(0, chunks, 2))
    owns = [(home_parity ^ parity(i)) == h for i in edges]
    edge_pairs = [(i, j) for i in range(REACH) for j in range(REACH - i)]
    reach_rows = REACH * rows

    def row_sums(near, at, left):
        blocks = lax.dynamic_slice_in_dim(near, at, REACH, 0).astype(jnp.float32)
        offset = lax.dynamic_slice_in_dim(near_offsets, at, REACH, 0)
        blocks = jnp.where(left, blocks[::-1], blocks)
        offset = jnp.where(left, -offset[::-1], offset)
        sums = []
        for row, source in edge_pairs:
            reads = (offset[row] == -(row + source + 1))[:, None, None]
            sums.append(jnp.sum(jnp.where(reads, blocks[row], 0.0), axis=0).astype(near.dtype))
        return sums

    def edge_sums(near, mine_too):
        sums = []
        for i, own in zip(edges, owns):
            left = own if mine_too else ~own
            sums += row_sums(near, (i + 1) * chunk - jnp.where(left, REACH, 0), left)
        return jnp.stack(sums)

    def side(device):
        return parity(device >> bits)

    def moved(other):
        other_parity = sum((((other >> bits) >> k) & 1) for k in range(chunks.bit_length())) & 1
        return (other >= 0) & (other < leafs) & (other_parity != home_parity)

    assert span > 1
    low_moved, high_moved = moved(d - 1), moved(d + 1)
    ends = [(a, a + 1) for a in range(leafs - 1) if side(a) != side(a + 1)]
    end_pairs = [(2 * a + side(a), 2 * a + 1 - side(a)) for pair in ends for a in pair]
    end_rows = jnp.where(high_moved, box_count - REACH, 0)

    half_pairs = chunk // 2
    pool = {
        "rhs": (rhs, chunk * rows, 0),
        "source": (source_t, chunk, 0),
        "source_blocks": (source_values, half_pairs, 1),
        "target": (target_t, chunk, 0),
        "target_blocks": (target_values, half_pairs, 1),
        "near": (near_t, chunk, 0),
    }
    arrays = {name: entry[0] for name, entry in pool.items()}
    queue = [(name, s) for s in range(steps) for name in ("rhs", "source", "source_blocks")]
    for s in range(steps):
        queue += [(name, s) for name in ("target_blocks", "target", "near")]
    queue += ["edges", "ends"]
    first_cut = pl.pallas_call(
        functools.partial(cut_kernel, span=span, masks=[masks[0][0], masks[1][0]]),
        out_shape=pltpu.VMEM((chunk * rows, columns), rhs.dtype),
        in_specs=[pl.BlockSpec(memory_space=pl.ANY)],
        out_specs=pl.BlockSpec(memory_space=pltpu.VMEM),
        scratch_shapes=[pltpu.SemaphoreType.DMA],
        name="first_cut",
    )
    both = ("leaf", "rhs")
    received = {}
    for n, entry in enumerate(queue):
        if entry == "edges":
            piece = edge_sums(arrays["near"], True)
        elif entry == "ends":
            piece = jnp.stack(row_sums(arrays["near"], end_rows, high_moved))
        else:
            name, s = entry
            piece = cut(arrays[name], others[s], pool[name][1], pool[name][2]) if n else first_cut(arrays[name])
        piece, arrays = lax.optimization_barrier((piece, arrays))
        received[entry] = lax.ppermute(piece, both, end_pairs) if entry == "ends" else swap(piece)

    peer_rhs = jnp.zeros(((box_count + 2 * REACH) * rows, columns), rhs.dtype)
    for s in range(steps):
        peer_rhs = lax.dynamic_update_slice_in_dim(
            peer_rhs, received["rhs", s], mine[s] * (chunk * rows) + reach_rows, 0
        )
    peer_tail = peer_rhs[box_count * rows : box_count * rows + reach_rows]
    peer_head = peer_rhs[reach_rows : 2 * reach_rows]
    up = [(i, i + 1) for i in range(leafs - 1)]
    down = [(i + 1, i) for i in range(leafs - 1)]
    ends_in = []
    for rows_out, way in ((arrays["rhs"][-reach_rows:], up), (arrays["rhs"][:reach_rows], down)):
        ends_in.append(lax.ppermute(rows_out, "leaf", way))
    for rows_out, way in ((peer_tail, up), (peer_head, down)):
        pairs = [(2 * a + side(a), 2 * b + side(b)) for a, b in way if side(a) == side(b)]
        ends_in.append(lax.ppermute(rows_out, both, pairs))
    low_own, high_own, low_peer, high_peer = ends_in
    peer_rhs = lax.dynamic_update_slice_in_dim(peer_rhs, low_peer, 0, 0)
    peer_rhs = lax.dynamic_update_slice_in_dim(peer_rhs, high_peer, box_count * rows + reach_rows, 0)
    own_rhs = jnp.concatenate([low_own, rhs, high_own], axis=0)

    params = pltpu.CompilerParams(
        dimension_semantics=("arbitrary",), vmem_limit_bytes=56 * 2**20
    )
    pair_count = group // 2
    wide = 2 * columns
    blocks_own = pl.BlockSpec(
        (levels, pair_count, 2, 2, half, rank), lambda t, i, *_: (0, i[0] * 2 + t, 0, 0, 0, 0)
    )
    blocks_peer = pl.BlockSpec((levels, pair_count, 2, 2, half, rank), lambda t, *_: (0, t, 0, 0, 0, 0))
    scale_spec = pl.BlockSpec(
        (levels, pair_count, 2, 2, rank), lambda t, i, *_: (0, i[0] * 2 + t, 0, 0, 0)
    )
    basis_own = pl.BlockSpec((group, half, rows), lambda t, i, *_: (i[0] * 2 + t, 0, 0))
    basis_peer = pl.BlockSpec((group, half, rows), lambda t, *_: (t, 0, 0))
    near_own = pl.BlockSpec((group, near_count, half, rows), lambda t, i, *_: (i[0] * 2 + t, 0, 0, 0))
    near_peer = pl.BlockSpec((group, near_count, half, rows), lambda t, *_: (t, 0, 0, 0))
    state_spec = pl.BlockSpec((group, rank, wide), lambda t, *_: (t, 0, 0))
    rhs_own = pl.BlockSpec((group * rows, columns), lambda t, i, *_: (i[0] * 2 + t, 0))
    rhs_peer = pl.BlockSpec((group * rows, columns), lambda t, *_: (t, 0))
    window_rows = (chunk + 2 * REACH) * rows
    window = pl.BlockSpec((window_rows, columns), lambda t, *_: (0, 0))
    weight_scratch = pltpu.VMEM((pair_count, 2 * rank, 2 * rank), rhs.dtype)
    state_scratch = pltpu.VMEM((group * rank, wide), rhs.dtype)

    rows_in = []
    for s in range(steps):
        index = jnp.stack([mine[s], h]).astype(jnp.int32)
        mixed = pl.pallas_call(
            source_kernel,
            out_shape=jax.ShapeDtypeStruct((chunk, rank, wide), rhs.dtype),
            grid_spec=pltpu.PrefetchScalarGridSpec(
                num_scalar_prefetch=1,
                grid=(2,),
                in_specs=[rhs_own, rhs_peer, basis_own, basis_peer, blocks_own, blocks_peer, scale_spec],
                out_specs=state_spec,
                scratch_shapes=[weight_scratch, state_scratch],
            ),
            compiler_params=params,
        )(index, rhs, received["rhs", s], source_t, received["source", s], source_values, received["source_blocks", s], source_scales)
        arrived = jnp.zeros((chunk, rank, wide), rhs.dtype)
        for k in range(span):
            slot = (d ^ k) & (span - 1)
            pairs = [
                (2 * a + e, 2 * (a ^ ((masks[e][s] << bits) | k)) + e) for a in range(leafs) for e in range(2)
            ]
            piece = lax.ppermute(cut(mixed, slot, quota), both, pairs)
            arrived = lax.dynamic_update_slice_in_dim(arrived, piece, slot * quota, 0)
        rows_in.append(arrived)

    offsets = near_offsets.reshape(-1)
    product = None
    returned = []
    for s in range(steps):
        index = jnp.stack([mine[s], h]).astype(jnp.int32)
        start = mine[s] * (chunk * rows)
        operands = [
            index, offsets, rows_in[s], target_values, received["target_blocks", s], target_scales,
            target_t, received["target", s], near_t, received["near", s],
            lax.dynamic_slice_in_dim(own_rhs, start, window_rows, 0),
            lax.dynamic_slice_in_dim(peer_rhs, start, window_rows, 0),
        ]
        specs = [
            state_spec, blocks_own, blocks_peer, scale_spec, basis_own, basis_peer, near_own, near_peer,
            window, window,
        ]
        aliases = {}
        if s:
            aliases = {len(operands): 0}
            operands.append(product)
            specs.append(pl.BlockSpec(memory_space=pl.ANY))
        far = pl.pallas_call(
            functools.partial(target_kernel, first=s == 0),
            out_shape=(
                jax.ShapeDtypeStruct((box_count * rows, columns), rhs.dtype),
                jax.ShapeDtypeStruct((chunk * rows, columns), rhs.dtype),
            ),
            grid_spec=pltpu.PrefetchScalarGridSpec(
                num_scalar_prefetch=2,
                grid=(2,),
                in_specs=specs,
                out_specs=(rhs_own, rhs_peer),
                scratch_shapes=[
                    weight_scratch,
                    state_scratch,
                    pltpu.VMEM((group, (near_count + 1) * 2 * half, rows), rhs.dtype),
                ],
            ),
            input_output_aliases=aliases,
            compiler_params=params,
        )
        product, send = far(*operands)
        at = others[s] * (chunk * rows)
        most = chunk * rows if s < steps - 1 else chunk * rows * 7 // 8
        for a, b in ((0, most), (most, chunk * rows)):
            if a < b:
                returned.append((swap(send[a:b]), at, a, b))

    own_sums = [edge_sums(near_t, False), jnp.stack(row_sums(near_t, end_rows, high_moved))]

    def products_of(own, peer, sources, left):
        sums = jnp.where(
            h == 0, jnp.concatenate([own, peer], axis=1), jnp.concatenate([peer, own], axis=1)
        )
        sources = sources.reshape(REACH, rows, columns)
        sources = jnp.where(left, sources[::-1], sources)
        products = [jnp.zeros((rows, columns), jnp.float32) for _ in range(REACH)]
        for p, (row, source) in enumerate(edge_pairs):
            products[row] += lax.dot_general(
                sums[p], sources[source], (((0,), (0,)), ((), ())), preferred_element_type=jnp.float32
            )
        products = jnp.stack(products)
        return jnp.where(left, products, products[::-1]).reshape(reach_rows, columns)

    count = len(edge_pairs)
    at_edges = []
    for n, (i, own) in enumerate(zip(edges, owns)):
        start = (i + 1) * chunk - jnp.where(own, REACH, 0)
        at_edges.append(
            products_of(
                own_sums[0][n * count : (n + 1) * count],
                received["edges"][n * count : (n + 1) * count],
                lax.dynamic_slice_in_dim(arrays["rhs"], start * rows, reach_rows, 0),
                own,
            )
        )
    at_edges = jnp.concatenate(at_edges, axis=0)
    at_end = products_of(
        own_sums[1], received["ends"], jnp.where(high_moved, high_own, low_own), ~high_moved
    )
    at_end = jnp.where((low_moved | high_moved) & (home_parity != h), at_end, 0.0)
    added = []
    for s in range(steps):
        inner = cut(at_edges, others[s] >> 1, reach_rows)
        first = jnp.where(others[s] & 1, inner, jnp.where((others[s] == 0) & ~high_moved, at_end, 0.0))
        last = jnp.where(others[s] & 1, jnp.where((others[s] == chunks - 1) & high_moved, at_end, 0.0), inner)
        middle = jnp.zeros(((chunk - 2 * REACH) * rows, columns), jnp.float32)
        added.append(jnp.concatenate([first, middle, last], axis=0))
    added = lax.optimization_barrier(added)
    for s, (part, at, a, b) in zip([*range(steps), steps - 1], returned):
        part = (part.astype(jnp.float32) + added[s][a:b]).astype(rhs.dtype)
        product = lax.dynamic_update_slice_in_dim(product, part, at + a, 0)
    return product


def solution(mesh):
    placed = (
        P("leaf", "rhs"),
        P("leaf", None, "rhs"),
        P("leaf", None, "rhs"),
        P("leaf", None, None, "rhs"),
        P("leaf", None),
        P(None, "leaf", None, None, "rhs", None),
        P(None, "leaf", None, None, None),
        P(None, "leaf", None, None, "rhs", None),
        P(None, "leaf", None, None, None),
    )
    return jax.shard_map(
        on_device, mesh=mesh, in_specs=placed, out_specs=P("leaf", "rhs"), check_vma=False
    )
```
